32 devices in a mesh: slides: 2 (over y), row: 16 (over z, x, core).
Axes of the slice: x: 2, y: 2, z: 4, core: 2. Of those that a mesh axis runs over, the one named last changes fastest.
Arguments:
- tiles: bfloat16 [7168, 16, 1024], P(('slides', 'row')), parts along dimension 0, may hold values from -6 to 6
- tile_mask: int32 [7168], P(('slides', 'row')), parts along dimension 0, may hold values from 0 to 1, as said below
- region_ids: int32 [7168], P(('slides', 'row')), parts along dimension 0, may hold values from 0 to 63
- w_reduce: bfloat16 [64, 64], replicated, may hold values from -0.75 to 0.75
- scale_reduce: float32 [64], replicated, may hold values from 0.5 to 1.5
- shift_reduce: float32 [64], replicated, may hold values from -3 to 3
- w_spatial: bfloat16 [576, 64], replicated, may hold values from -0.25 to 0.25
- scale_spatial: float32 [64], replicated, may hold values from 0.5 to 1.5
- shift_spatial: float32 [64], replicated, may hold values from -3 to 3
- w_expand: bfloat16 [64, 256], replicated, may hold values from -0.75 to 0.75
- scale_expand: float32 [256], replicated, may hold values from 0.5 to 1.5
- shift_expand: float32 [256], replicated, may hold values from -3 to 3
- w_project: bfloat16 [64, 256], replicated, may hold values from -0.75 to 0.75
- scale_project: float32 [256], replicated, may hold values from 0.5 to 1.5
- shift_project: float32 [256], replicated, may hold values from -3 to 3
Outputs:
- tile_features: bfloat16 [7168, 256], P(('slides', 'row')), parts along dimension 0
- region_means: float32 [128, 256], P(('slides', 'row')), parts along dimension 0
The draws below stay inside these ranges and needn't reach their ends.
There are 2 independent parts, one for each index of `slides`. The reference program is written for one: setup_inputs(seed, part) draws one part's arguments, and reference() takes and returns one part's arrays. A program takes and returns all parts, laid end to end along the dimension named above; an argument that names none is the same for every part. Nothing has to cross between parts.
Inputs may be any that keep to these rules, and one draw needn't show every extreme that they name: `tile_mask`: every band of 224 consecutive slots holds at least 96 and at most 224 tissue tiles, and some band holds exactly 224. The slide holds exactly (160) times the number of bands tissue tiles.
All inputs are finite; a program needn't handle non-finite values.
Results may differ from the reference program's by a relative error of at most 0.002.
Values may be sent and summed in bfloat16 or wider, within the bound.
A program may use at most 64 MiB of HBM per device.

```python
import math
import jax
import jax.numpy as jnp
import numpy as np
from jax import lax

C_IN = 64
C_MID = 64
C_OUT = 256
SIDE = 16
KEEP = 96
SHARE = 64
TILE_DEV = 224
TILES = 3584
REGIONS = 64
N_ROW = 16


def draw_tile_mask(key, part):
    key_level, key_step, key_order, key_slots = jax.random.split(key, 4)
    level = jax.random.randint(key_level, (N_ROW,), 0, SHARE + 1)
    step_by = jax.random.randint(key_step, (), 1, N_ROW)
    level = level.at[0].set(SHARE).at[step_by].set(0)
    later = jnp.take(level, (jnp.arange(N_ROW) + step_by) % N_ROW)
    excess = SHARE + level - later
    excess = jnp.take(excess, jax.random.permutation(key_order, N_ROW))
    tissue = KEEP + excess
    slot_keys = jax.random.split(key_slots, N_ROW)
    orders = jax.vmap(lambda each_key: jax.random.permutation(each_key, TILE_DEV))(slot_keys)
    return (orders < tissue[:, None]).astype(jnp.int32).reshape(-1)


def touch_ends(result, stream_key, low, top_value):
    index_at = [jax.random.randint(jax.random.fold_in(stream_key, axis), (), 0, length) for axis, length in enumerate(result.shape)]
    longest = result.shape.index(max(result.shape))
    neighbour = index_at[:longest] + [(index_at[longest] + 1) % result.shape[longest]] + index_at[longest + 1:]
    return result.at[tuple(index_at)].set(low).at[tuple(neighbour)].set(top_value)


def block_scale(stream_key, shape, pieces, low, largest):
    def one(position, shards_of):
        heights = jax.random.uniform(jax.random.fold_in(jax.random.fold_in(stream_key, 6), position), (shards_of,), jnp.float32, low / len(pieces), largest / len(pieces))
        return jnp.repeat(jnp.exp(heights), shape[position] // shards_of).reshape((-1,) + (1,) * (len(shape) - position - 1))

    gain = one(*pieces[0])
    for cut in pieces[1:]:
        gain = gain * one(*cut)
    return gain


def rank_bounds(amount, slope):
    portions = [(1 << 20) // math.isqrt(rank ** slope) + 1 for rank in range(1, amount + 1)]
    spread = 1 + sum(portions) // (1 << 30)
    return np.cumsum(np.array([max(1, weight // spread) for weight in portions]))


def ranked_ids(key, dims, amount, slope):
    table = rank_bounds(amount, slope)
    pick = jax.random.randint(jax.random.fold_in(key, 1), dims, 0, int(table[amount - 1]))
    grade = jnp.searchsorted(jnp.asarray(table, jnp.int32), pick, side="right")
    return jax.random.permutation(jax.random.fold_in(key, 2), amount)[grade].astype(jnp.int32)


def noise(rng, shape, scale, reach, cuts=(), held_as=jnp.bfloat16):
    level = block_scale(rng, shape, cuts, -0.22, 0.18) if cuts else 1.0
    drawn = jax.random.normal(rng, shape, jnp.float32) * scale * level
    return jnp.minimum(jnp.maximum(drawn, -reach), reach).astype(held_as)


def setup_inputs(seed: int = 0, part: int = 0) -> dict:
    streams_of = jax.random.split(jax.random.key(seed), 16)
    part_keys = jax.random.split(jax.random.fold_in(streams_of[15], part), 16)
    return {
        "tiles": noise(part_keys[0], (TILES, SIDE, SIDE * C_IN), 1.0, 6.0, ((0, 16),)),
        "tile_mask": draw_tile_mask(jax.random.fold_in(jax.random.fold_in(streams_of[15], part), 71), part),
        "region_ids": touch_ends(ranked_ids(part_keys[2], (TILES,), REGIONS, 2), jax.random.fold_in(part_keys[2], 3), 0, REGIONS - 1).astype(jnp.int32),
        "w_reduce": noise(streams_of[3], (C_IN, C_MID), C_IN ** -0.5, 0.75),
        "scale_reduce": jnp.clip(jax.random.uniform(streams_of[4], (C_MID,), jnp.float32, 0.5, 1.5), 0.5, 1.5),
        "shift_reduce": noise(streams_of[5], (C_MID,), 0.5, 3.0, (), jnp.float32),
        "w_spatial": noise(streams_of[6], (9 * C_MID, C_MID), (9 * C_MID) ** -0.5, 0.25),
        "scale_spatial": jnp.clip(jax.random.uniform(streams_of[7], (C_MID,), jnp.float32, 0.5, 1.5), 0.5, 1.5),
        "shift_spatial": noise(streams_of[8], (C_MID,), 0.5, 3.0, (), jnp.float32),
        "w_expand": noise(streams_of[9], (C_MID, C_OUT), C_MID ** -0.5, 0.75),
        "scale_expand": jnp.clip(jax.random.uniform(streams_of[10], (C_OUT,), jnp.float32, 0.5, 1.5), 0.5, 1.5),
        "shift_expand": noise(streams_of[11], (C_OUT,), 0.5, 3.0, (), jnp.float32),
        "w_project": noise(streams_of[12], (C_IN, C_OUT), C_IN ** -0.5, 0.75),
        "scale_project": jnp.clip(jax.random.uniform(streams_of[13], (C_OUT,), jnp.float32, 0.5, 1.5), 0.5, 1.5),
        "shift_project": noise(streams_of[14], (C_OUT,), 0.5, 3.0, (), jnp.float32),
    }


def pick_block(num_rows):
    for size in (16, 8, 4, 2, 1):
        if num_rows % size == 0:
            return size
    return 1


def block_features(group, w_reduce, scale_reduce, shift_reduce, w_spatial, scale_spatial, shift_spatial, w_expand, scale_expand, shift_expand, w_project, scale_project, shift_project):
    count_tiles = group.shape[0]
    side = group.shape[1]
    c_in = w_reduce.shape[0]
    c_mid = w_reduce.shape[1]
    c_out = w_expand.shape[1]
    inputs = group.reshape(count_tiles * side * side, c_in)
    reduced = jnp.maximum(jnp.dot(inputs, w_reduce, preferred_element_type=jnp.float32) * scale_reduce + shift_reduce, 0.0).astype(jnp.bfloat16)
    grid = reduced.reshape(count_tiles, side, side, c_mid)
    padded = jnp.pad(grid, ((0, 0), (1, 1), (1, 1), (0, 0)))
    total = jnp.zeros((count_tiles * side * side, c_mid), jnp.float32)
    for row_off in range(3):
        for col_off in range(3):
            window = padded[:, row_off:row_off + side, col_off:col_off + side, :].reshape(-1, c_mid)
            start = (3 * row_off + col_off) * c_mid
            total = total + jnp.dot(window, w_spatial[start:start + c_mid], preferred_element_type=jnp.float32)
    spatial = jnp.maximum(total * scale_spatial + shift_spatial, 0.0).astype(jnp.bfloat16)
    expanded = jnp.dot(spatial, w_expand, preferred_element_type=jnp.float32) * scale_expand + shift_expand
    shortcut = jnp.dot(inputs, w_project, preferred_element_type=jnp.float32) * scale_project + shift_project
    combined = jnp.maximum(expanded + shortcut, 0.0)
    return jnp.mean(combined.reshape(count_tiles, side * side, c_out), axis=1)


def reference(tiles, tile_mask, region_ids, w_reduce, scale_reduce, shift_reduce, w_spatial, scale_spatial, shift_spatial, w_expand, scale_expand, shift_expand, w_project, scale_project, shift_project):
    params = (w_reduce, scale_reduce, shift_reduce, w_spatial, scale_spatial, shift_spatial, w_expand, scale_expand, shift_expand, w_project, scale_project, shift_project)
    total_live = N_ROW * (KEEP + SHARE)
    live_index = jnp.nonzero(tile_mask, size=total_live)[0].astype(jnp.int32)
    block_size = pick_block(total_live)
    blocks = live_index.reshape(total_live // block_size, block_size)

    def run(index_block):
        return block_features(jnp.take(tiles, index_block, axis=0), *params)

    pooled = lax.map(run, blocks).reshape(total_live, C_OUT)
    tile_features = jnp.zeros((TILES, C_OUT), jnp.bfloat16).at[live_index].set(pooled.astype(jnp.bfloat16))
    sums = jax.ops.segment_sum(tile_features.astype(jnp.float32), region_ids, num_segments=REGIONS)
    counts = jax.ops.segment_sum(tile_mask.astype(jnp.float32), region_ids, num_segments=REGIONS)
    region_means = sums / jnp.maximum(counts, 1.0)[:, None]
    return tile_features, region_means
```

```python
import functools

import jax
import jax.numpy as jnp
from jax import lax
from jax.experimental import pallas as pl
from jax.experimental.pallas import tpu as pltpu
from jax.sharding import PartitionSpec as P

BLOCK = 32
VMEM_LIMIT = 58 * 1024 * 1024
F32 = jnp.float32
BF16 = jnp.bfloat16


def pick_block(slots):
    for size in (BLOCK, 16, 8, 4, 2):
        if slots % size == 0:
            return size
    return 1


def across(blocks):
    return jnp.concatenate(blocks, axis=1)


def prepare(raw, wr_ref, ws_ref, wo_ref, vec_ref, positions):
    wred, sred, hred, wspa, sspa, hspa, wexp, sexp, hexp, wpro, spro, hpro = raw
    none = jnp.zeros((64, 64), BF16)
    w = wred[...]
    for i in range(4):
        wr_ref[64 * i : 64 * i + 64, :] = across([w if i == j else none for j in range(4)])
    turned = wspa[...].T
    columns = (0, 1, 2, -1)
    for d in range(4):
        for k in range(4):
            line = []
            for n in range(4):
                i, j = d - n // 2, columns[k] - n % 2 + 1
                inside = 0 <= i < 3 and 0 <= j < 3
                at = 64 * (3 * i + j)
                line.append(turned[at : at + 64, :] if inside else none)
            ws_ref[d, 64 * k : 64 * k + 64, :] = across(line)
    ratio = wpro[...].astype(F32) * (spro[...] / sexp[...])
    high = ratio.astype(BF16)
    rest = (ratio - high.astype(F32)).astype(BF16)
    blank = jnp.zeros((64, 256), BF16)
    for n in range(2):
        wo_ref[n, 0:64, :] = wexp[...] if n == 0 else blank
        wo_ref[n, 64:128, :] = blank if n == 0 else wexp[...]
        wo_ref[n, 128:192, :] = high
        wo_ref[n, 192:256, :] = rest
    shift = hexp[...] + hpro[...]
    vec_ref[0:1, :] = across([sred[...]] * 4)
    vec_ref[1:2, :] = across([hred[...]] * 4)
    vec_ref[2:3, :] = across([sspa[...]] * 4)
    vec_ref[3:4, :] = across([hspa[...]] * 4)
    vec_ref[4:5, :] = -shift / sexp[...]
    vec_ref[5:6, :] = sexp[...] * (1.0 / positions)
    vec_ref[6:7, :] = shift


def block_kernel(devices, *refs):
    x_ref, mask_ref, ids_ref = refs[0:3]
    raw = refs[3:15]
    feat_ref, mean_ref = refs[15:17]
    wr_ref, ws_ref, wo_ref, vec_ref, red_ref, spa_ref, mcol_ref = refs[17:24]
    part_ref, land_ref, send_sem, recv_sem = refs[24:28]
    step = pl.program_id(0)
    steps = pl.num_programs(0)
    nt, side, width = x_ref.shape
    pairs = width // 128
    rows = nt * side
    half = rows // 2
    slots = feat_ref.shape[0]
    me = lax.axis_index("row")
    barrier = pltpu.get_barrier_semaphore()

    def peer(turn):
        return lax.rem(me + turn, devices)

    @pl.when(step == 0)
    def _():
        def greet(turn, carry):
            pl.semaphore_signal(
                barrier, inc=1, device_id={"row": peer(turn)}, device_id_type=pl.DeviceIdType.MESH
            )
            return carry

        lax.fori_loop(1, devices, greet, 0)
        red_ref[:, :, 0:8, :] = jnp.zeros((pairs, nt, 8, 128), F32)
        red_ref[:, :, 24:32, :] = jnp.zeros((pairs, nt, 8, 128), F32)
        row = lax.broadcasted_iota(jnp.int32, (slots, slots), 0)
        col = lax.broadcasted_iota(jnp.int32, (slots, slots), 1)
        diag = jnp.where(row == col, mask_ref[...].astype(F32), 0.0).astype(BF16)
        mcol_ref[...] = jnp.dot(diag, jnp.ones((slots, 128), BF16), preferred_element_type=F32)
        prepare(raw, wr_ref, ws_ref, wo_ref, vec_ref, side * side)

    x = x_ref[...].reshape(rows, width)
    scale_r, shift_r = vec_ref[0:1, :], vec_ref[1:2, :]
    scale_s, shift_s = vec_ref[2:3, :], vec_ref[3:4, :]
    floor, scale_o, shift_o = vec_ref[4:5, :], vec_ref[5:6, :], vec_ref[6:7, :]

    for g in range(pairs // 2):
        r = jnp.dot(x[:, 256 * g : 256 * g + 256], wr_ref[...], preferred_element_type=F32)
        r = jnp.maximum(r * scale_r + shift_r, 0.0)
        for h in range(2):
            red_ref[2 * g + h, :, 8 : 8 + side, :] = r[:, 128 * h : 128 * h + 128].reshape(
                nt, side, 128
            )

    low = lax.broadcasted_iota(jnp.int32, (half, 128), 1) < 64
    tall = [
        [
            red_ref[p, :, pl.ds(7 + d, 8, stride=2), :].reshape(half, 128).astype(BF16)
            for d in range(4)
        ]
        for p in range(pairs)
    ]
    zero = jnp.zeros((half, 128), BF16)
    for p in range(pairs):
        acc = None
        for d in range(4):
            after = tall[p + 1][d] if p + 1 < pairs else zero
            before = tall[p - 1][d] if p > 0 else zero
            lhs = across([tall[p][d], jnp.where(low, after, before)])
            term = jnp.dot(lhs, ws_ref[d], preferred_element_type=F32)
            acc = term if acc is None else acc + term
        s = jnp.maximum(acc * scale_s + shift_s, 0.0)
        spa_ref[p, pl.ds(0, half, stride=2), :] = s[:, 0:128]
        spa_ref[p, pl.ds(1, half, stride=2), :] = s[:, 128:256]

    low = lax.broadcasted_iota(jnp.int32, (rows, 128), 1) < 64
    total = jnp.zeros((rows, 256), F32)
    for p in range(pairs):
        xp = x[:, 128 * p : 128 * p + 128]
        xr = across([xp[:, 64:128], xp[:, 0:64]])
        sp = spa_ref[p].astype(BF16)
        first = across([sp, jnp.where(low, xp, xr)])
        second = across([sp, jnp.where(low, xr, xp)])
        z0 = jnp.dot(first, wo_ref[0], preferred_element_type=F32)
        z1 = jnp.dot(second, wo_ref[1], preferred_element_type=F32)
        total = total + (jnp.maximum(z0, floor) + jnp.maximum(z1, floor))
    pooled = jnp.sum(total.reshape(nt, side, 256), axis=1)
    pooled = pooled * scale_o + shift_o
    at = pl.multiple_of(step * nt, nt)
    keep = mcol_ref[pl.ds(at, nt), :]
    feat_ref[pl.ds(at, nt), :] = (pooled * across([keep, keep])).astype(BF16)

    @pl.when(step == steps - 1)
    def _():
        row = lax.broadcasted_iota(jnp.int32, (8 * devices, slots), 0)
        region = row // 8 * 4 + row % 4
        member = jnp.where(region == ids_ref[...], 1.0, 0.0).astype(BF16)
        sums = jnp.dot(member, feat_ref[...], preferred_element_type=F32)
        counts = jnp.dot(member, mcol_ref[...].astype(BF16), preferred_element_type=F32)
        place = lax.broadcasted_iota(jnp.int32, (8 * devices, 128), 0) % 8
        lane = lax.broadcasted_iota(jnp.int32, (8 * devices, 128), 1)
        sums = jnp.where(place < 4, sums[:, 0:128], sums[:, 128:256])
        counts = jnp.where(place == lane, counts, 0.0).reshape(devices, 8, 128)
        part_ref[:, 0:8, :] = sums.reshape(devices, 8, 128)
        part_ref[:, 8:9, :] = jnp.sum(counts, axis=1, keepdims=True)
        pl.semaphore_wait(barrier, devices - 1)

        def send(turn, carry):
            pltpu.make_async_remote_copy(
                src_ref=part_ref.at[peer(turn)],
                dst_ref=land_ref.at[turn],
                send_sem=send_sem,
                recv_sem=recv_sem,
                device_id={"row": peer(turn)},
                device_id_type=pl.DeviceIdType.MESH,
            ).start()
            return carry

        lax.fori_loop(1, devices, send, 0)
        land_ref[0] = part_ref[me]
        others = land_ref.at[pl.ds(1, devices - 1)]
        pltpu.make_async_copy(others, others, recv_sem).wait()
        landed = jnp.sum(land_ref[...], axis=0)
        row = lax.broadcasted_iota(jnp.int32, (8, 128), 0) % 4
        lane = lax.broadcasted_iota(jnp.int32, (8, 128), 1)
        count = jnp.sum(
            jnp.where(row == lane, landed[8:9], 0.0), axis=1, keepdims=True
        )
        means = landed[0:8] / jnp.maximum(count, 1.0)
        mean_ref[:, 0:128] = means[0:4]
        mean_ref[:, 128:256] = means[4:8]
        sent = part_ref.at[pl.ds(1, devices - 1)]
        pltpu.make_async_copy(sent, sent, send_sem).wait()


def body(tiles, tile_mask, region_ids, *params, devices):
    slots, side, width = tiles.shape
    c_out = params[6].shape[1]
    nt = pick_block(slots)
    whole = lambda shape: pl.BlockSpec(shape, lambda i: (0,) * len(shape))
    flat = [p if p.ndim == 2 else p.reshape(1, -1) for p in params]
    flat[3] = params[3].T
    return pl.pallas_call(
        functools.partial(block_kernel, devices),
        grid=(slots // nt,),
        in_specs=[
            pl.BlockSpec((nt, side, width), lambda i: (i, 0, 0)),
            whole((1, slots)),
            whole((1, slots)),
        ]
        + [whole(p.shape) for p in flat],
        out_specs=[whole((slots, c_out)), whole((4, c_out))],
        out_shape=[
            pltpu.VMEM((slots, c_out), BF16),
            pltpu.VMEM((4, c_out), F32),
        ],
        scratch_shapes=[
            pltpu.VMEM((256, 256), BF16),
            pltpu.VMEM((4, 256, 256), BF16),
            pltpu.VMEM((2, 256, 256), BF16),
            pltpu.VMEM((8, 256), F32),
            pltpu.VMEM((width // 128, nt, 32, 128), F32),
            pltpu.VMEM((width // 128, nt * side, 128), F32),
            pltpu.VMEM((slots, 128), F32),
            pltpu.VMEM((devices, 9, 128), F32),
            pltpu.VMEM((devices, 9, 128), F32),
            pltpu.SemaphoreType.DMA,
            pltpu.SemaphoreType.DMA,
        ],
        compiler_params=pltpu.CompilerParams(
            vmem_limit_bytes=VMEM_LIMIT, collective_id=0, has_side_effects=True
        ),
        name="block_features",
    )(tiles, tile_mask.reshape(1, slots), region_ids.reshape(1, slots), *flat)


def solution(mesh):
    devices = mesh.shape["row"]
    split = P(("slides", "row"))
    return jax.shard_map(
        functools.partial(body, devices=devices),
        mesh=mesh,
        in_specs=(P(("slides", "row"), None, None), split, split) + (P(),) * 12,
        out_specs=(P(("slides", "row"), None), P(("slides", "row"), None)),
        check_vma=False,
    )
```

```python
import functools

import jax
import jax.numpy as jnp
from jax import lax
from jax.experimental import pallas as pl
from jax.experimental.pallas import tpu as pltpu
from jax.sharding import PartitionSpec as P

BLOCK = 32
VMEM_LIMIT = 58 * 1024 * 1024
F32 = jnp.float32
BF16 = jnp.bfloat16


def pick_block(slots):
    for size in (BLOCK, 16):
        if slots % size == 0:
            return size
    return slots


def across(blocks):
    return jnp.concatenate(blocks, axis=1)


def prepare(raw, wr_ref, ws_ref, wb_ref, wo_ref, vec_ref, positions):
    wred, sred, hred, wspa, sspa, hspa, wexp, sexp, hexp, wpro, spro, hpro = raw
    none = jnp.zeros((64, 64), BF16)
    w = wred[...]
    for i in range(4):
        wr_ref[64 * i : 64 * i + 64, :] = across([w if i == j else none for j in range(4)])
    turned = wspa[...].T

    def line(d, column):
        blocks = []
        for n in range(4):
            i, j = d - n // 2, column - n % 2 + 1
            at = 64 * (3 * i + j)
            inside = 0 <= i < 3 and 0 <= j < 3
            blocks.append(turned[at : at + 64, :] if inside else none)
        return across(blocks)

    for d in range(4):
        for k, column in enumerate((0, 1, 2, -1)):
            ws_ref[d, 64 * k : 64 * k + 64, :] = line(d, column)
    for t in range(2):
        for k in range(4):
            wb_ref[t, 64 * k : 64 * k + 64, :] = line(2 * t + k // 2, k % 2)
    for t, column in ((2, 2), (3, -1)):
        for d in range(4):
            wb_ref[t, 64 * d : 64 * d + 64, :] = line(d, column)
    ratio = wpro[...].astype(F32) * (spro[...] / sexp[...])
    high = ratio.astype(BF16)
    rest = (ratio - high.astype(F32)).astype(BF16)
    blank = jnp.zeros((64, 256), BF16)
    for n in range(2):
        wo_ref[n, 0:64, :] = wexp[...] if n == 0 else blank
        wo_ref[n, 64:128, :] = blank if n == 0 else wexp[...]
        wo_ref[n, 128:192, :] = high
        wo_ref[n, 192:256, :] = rest
    shift = hexp[...] + hpro[...]
    vec_ref[0:1, :] = across([sred[...]] * 4)
    vec_ref[1:2, :] = across([hred[...]] * 4)
    vec_ref[2:3, :] = across([sspa[...]] * 4)
    vec_ref[3:4, :] = across([hspa[...]] * 4)
    vec_ref[4:5, :] = -shift / sexp[...]
    vec_ref[5:6, :] = sexp[...] * (1.0 / positions)
    vec_ref[6:7, :] = shift


def block_kernel(devices, nt, *refs):
    tiles_ref = refs[0]
    flat = refs[1:15]
    feat_ref, mean_ref = refs[15:17]
    held = refs[17:31]
    x_ref, wr_ref, ws_ref, wb_ref, wo_ref, vec_ref = refs[31:37]
    red_ref, spa_ref, mcol_ref, member_ref = refs[37:41]
    pooled_ref = refs[47]
    part_ref, land_ref, tile_sem, flat_sem, send_sem, recv_sem = refs[41:47]
    slots, side, width = tiles_ref.shape
    steps = slots // nt
    pairs = width // 128
    rows = nt * side
    half = rows // 2
    me = lax.axis_index("row")
    barrier = pltpu.get_barrier_semaphore()

    def peer(turn):
        return lax.rem(me + turn, devices)

    def tile_copy(step):
        at = pl.ds(pl.multiple_of(step * nt, nt), nt)
        return pltpu.make_async_copy(tiles_ref.at[at], x_ref.at[at], tile_sem.at[step])

    copies = [
        pltpu.make_async_copy(flat[n], held[n], flat_sem.at[n]) for n in range(len(flat))
    ]
    for copy in copies[2:]:
        copy.start()
    tile_copy(0).start()
    for copy in copies[:2]:
        copy.start()
    tile_copy(1).start()

    def greet(turn, carry):
        pl.semaphore_signal(
            barrier, inc=1, device_id={"row": peer(turn)}, device_id_type=pl.DeviceIdType.MESH
        )
        return carry

    lax.fori_loop(1, devices, greet, 0)
    for copy in copies:
        copy.wait()
    mask_ref, ids_ref = held[0:2]
    prepare(held[2:], wr_ref, ws_ref, wb_ref, wo_ref, vec_ref, side * side)
    row = lax.broadcasted_iota(jnp.int32, (slots, slots), 0)
    col = lax.broadcasted_iota(jnp.int32, (slots, slots), 1)
    diag = jnp.where(row == col, mask_ref[...].astype(F32), 0.0).astype(BF16)
    mcol_ref[...] = jnp.dot(diag, jnp.ones((slots, 128), BF16), preferred_element_type=F32)
    row = lax.broadcasted_iota(jnp.int32, (8 * devices, slots), 0)
    region = row // 8 * 4 + row % 4
    member = jnp.where(region == ids_ref[...], 1.0, 0.0).astype(BF16)
    member_ref[...] = member
    counts = jnp.dot(member, mcol_ref[...].astype(BF16), preferred_element_type=F32)
    place = lax.broadcasted_iota(jnp.int32, (8 * devices, 128), 0) % 8
    lane = lax.broadcasted_iota(jnp.int32, (8 * devices, 128), 1)
    counts = jnp.where(place == lane, counts, 0.0).reshape(devices, 8, 128)
    part_ref[:, 8:9, :] = jnp.sum(counts, axis=1, keepdims=True)

    scale_r, shift_r = vec_ref[0:1, :], vec_ref[1:2, :]
    scale_s, shift_s = vec_ref[2:3, :], vec_ref[3:4, :]
    floor, scale_o, shift_o = vec_ref[4:5, :], vec_ref[5:6, :], vec_ref[6:7, :]

    def block(step, carry):
        tile_copy(step).wait()

        @pl.when(step + 2 < steps)
        def _():
            tile_copy(step + 2).start()

        at = pl.ds(pl.multiple_of(step * nt, nt), nt)
        x = x_ref[at].reshape(rows, width)
        for g in range(pairs // 2):
            r = jnp.dot(x[:, 256 * g : 256 * g + 256], wr_ref[...], preferred_element_type=F32)
            r = jnp.maximum(r * scale_r + shift_r, 0.0)
            for h in range(2):
                red_ref[2 * g + h, :, 8 : 8 + side, :] = r[:, 128 * h : 128 * h + 128].reshape(
                    nt, side, 128
                )

        low = lax.broadcasted_iota(jnp.int32, (half, 128), 1) < 64
        tall = [
            [
                red_ref[p, :, pl.ds(7 + d, 8, stride=2), :].reshape(half, 128).astype(BF16)
                for d in range(4)
            ]
            for p in range(pairs)
        ]
        def swap(v):
            return across([v[:, 64:128], v[:, 0:64]])

        def side_of(p, d):
            if p == 0:
                return jnp.where(low, tall[1][d], swap(tall[1][d + 1]))
            return jnp.where(low, swap(tall[p - 1][d]), tall[p - 1][d + 1])

        for p in range(pairs):
            if 0 < p < pairs - 1:
                lhs = [
                    across([tall[p][d], jnp.where(low, tall[p + 1][d], tall[p - 1][d])])
                    for d in range(4)
                ]
                weights = [ws_ref[d] for d in range(4)]
            else:
                lhs = [across([tall[p][d], tall[p][d + 1]]) for d in (0, 2)]
                lhs.append(across([side_of(p, 0), side_of(p, 2)]))
                weights = [wb_ref[0], wb_ref[1], wb_ref[2 + int(p > 0)]]
            acc = None
            for v, w in zip(lhs, weights):
                term = jnp.dot(v, w, preferred_element_type=F32)
                acc = term if acc is None else acc + term
            s = jnp.maximum(acc * scale_s + shift_s, 0.0)
            spa_ref[p, pl.ds(0, half, stride=2), :] = s[:, 0:128]
            spa_ref[p, pl.ds(1, half, stride=2), :] = s[:, 128:256]

        group = 8
        deep = group * side
        low = lax.broadcasted_iota(jnp.int32, (deep, 128), 1) < 64
        for part in range(nt // group):
            r = slice(deep * part, deep * part + deep)
            first, second = [], []
            for p in range(pairs):
                xp = x[r, 128 * p : 128 * p + 128]
                xr = across([xp[:, 64:128], xp[:, 0:64]])
                sp = spa_ref[p, r, :].astype(BF16)
                first.append(across([sp, jnp.where(low, xp, xr)]))
                second.append(across([sp, jnp.where(low, xr, xp)]))
            z0 = jnp.dot(
                jnp.concatenate(first, axis=0), wo_ref[0], preferred_element_type=F32
            )
            z1 = jnp.dot(
                jnp.concatenate(second, axis=0), wo_ref[1], preferred_element_type=F32
            )
            total = None
            for p in range(pairs):
                q = slice(deep * p, deep * p + deep)
                z = jnp.maximum(z0[q], floor) + jnp.maximum(z1[q], floor)
                total = z if total is None else total + z
            pooled = jnp.sum(total.reshape(group, side, 256), axis=1)
            pooled_ref[group * part : group * part + group, :] = pooled
        keep = mcol_ref[at, :]
        pooled = (pooled_ref[...] * scale_o + shift_o) * across([keep, keep])
        feat_ref[at, :] = pooled.astype(BF16)
        return carry

    red_ref[:, :, 0:8, :] = jnp.zeros((pairs, nt, 8, 128), F32)
    red_ref[:, :, 24:32, :] = jnp.zeros((pairs, nt, 8, 128), F32)
    lax.fori_loop(0, steps, block, 0)

    sums = jnp.dot(member_ref[...], feat_ref[...], preferred_element_type=F32)
    sums = jnp.where(place < 4, sums[:, 0:128], sums[:, 128:256])
    part_ref[:, 0:8, :] = sums.reshape(devices, 8, 128)
    pl.semaphore_wait(barrier, devices - 1)

    def send(turn, carry):
        pltpu.make_async_remote_copy(
            src_ref=part_ref.at[peer(turn)],
            dst_ref=land_ref.at[turn],
            send_sem=send_sem,
            recv_sem=recv_sem,
            device_id={"row": peer(turn)},
            device_id_type=pl.DeviceIdType.MESH,
        ).start()
        return carry

    lax.fori_loop(1, devices, send, 0)
    land_ref[0] = part_ref[me]
    others = land_ref.at[pl.ds(1, devices - 1)]
    pltpu.make_async_copy(others, others, recv_sem).wait()
    landed = jnp.sum(land_ref[...], axis=0)
    row = lax.broadcasted_iota(jnp.int32, (8, 128), 0) % 4
    lane = lax.broadcasted_iota(jnp.int32, (8, 128), 1)
    count = jnp.sum(jnp.where(row == lane, landed[8:9], 0.0), axis=1, keepdims=True)
    means = landed[0:8] / jnp.maximum(count, 1.0)
    mean_ref[:, 0:128] = means[0:4]
    mean_ref[:, 128:256] = means[4:8]
    sent = part_ref.at[pl.ds(1, devices - 1)]
    pltpu.make_async_copy(sent, sent, send_sem).wait()


def body(tiles, tile_mask, region_ids, *params, devices):
    slots, side, width = tiles.shape
    c_out = params[6].shape[1]
    nt = pick_block(slots)
    pairs = width // 128
    flat = [p if p.ndim == 2 else p.reshape(1, -1) for p in params]
    flat[3] = params[3].T
    flat = [tile_mask.reshape(1, slots), region_ids.reshape(1, slots)] + flat
    return pl.pallas_call(
        functools.partial(block_kernel, devices, nt),
        in_specs=[pl.BlockSpec(memory_space=pltpu.HBM)] * (1 + len(flat)),
        out_specs=[pl.BlockSpec(memory_space=pltpu.VMEM)] * 2,
        out_shape=[pltpu.VMEM((slots, c_out), BF16), pltpu.VMEM((4, c_out), F32)],
        scratch_shapes=[pltpu.VMEM(p.shape, p.dtype) for p in flat]
        + [
            pltpu.VMEM((slots, side, width), BF16),
            pltpu.VMEM((256, 256), BF16),
            pltpu.VMEM((4, 256, 256), BF16),
            pltpu.VMEM((4, 256, 256), BF16),
            pltpu.VMEM((2, 256, 256), BF16),
            pltpu.VMEM((8, 256), F32),
            pltpu.VMEM((pairs, nt, side + 16, 128), F32),
            pltpu.VMEM((pairs, nt * side, 128), F32),
            pltpu.VMEM((slots, 128), F32),
            pltpu.VMEM((8 * devices, slots), BF16),
            pltpu.VMEM((devices, 9, 128), F32),
            pltpu.VMEM((devices, 9, 128), F32),
            pltpu.SemaphoreType.DMA((slots // nt,)),
            pltpu.SemaphoreType.DMA((len(flat),)),
            pltpu.SemaphoreType.DMA,
            pltpu.SemaphoreType.DMA,
            pltpu.VMEM((nt, 256), F32),
        ],
        compiler_params=pltpu.CompilerParams(
            vmem_limit_bytes=VMEM_LIMIT, collective_id=0, has_side_effects=True
        ),
        name="block_features",
    )(tiles, *flat)


def solution(mesh):
    devices = mesh.shape["row"]
    split = P(("slides", "row"))
    return jax.shard_map(
        functools.partial(body, devices=devices),
        mesh=mesh,
        in_specs=(P(("slides", "row"), None, None), split, split) + (P(),) * 12,
        out_specs=(P(("slides", "row"), None), P(("slides", "row"), None)),
        check_vma=False,
    )
```

```python
import functools

import jax
import jax.numpy as jnp
from jax import lax
from jax.experimental import pallas as pl
from jax.experimental.pallas import tpu as pltpu
from jax.sharding import PartitionSpec as P

BLOCK = 32
VMEM_LIMIT = 58 * 1024 * 1024
F32 = jnp.float32
BF16 = jnp.bfloat16


def pick_block(slots):
    for size in (BLOCK, 16):
        if slots % size == 0:
            return size
    return slots


def across(blocks):
    return jnp.concatenate(blocks, axis=1)


def prepare(raw, wr_ref, ws_ref, wb_ref, wo_ref, vec_ref, positions):
    wred, sred, hred, wspa, sspa, hspa, wexp, sexp, hexp, wpro, spro, hpro = raw
    none = jnp.zeros((64, 64), BF16)
    w = wred[...]
    for i in range(4):
        wr_ref[64 * i : 64 * i + 64, :] = across([w if i == j else none for j in range(4)])
    turned = wspa[...].T

    def line(d, column):
        blocks = []
        for n in range(4):
            i, j = d - n // 2, column - n % 2 + 1
            at = 64 * (3 * i + j)
            inside = 0 <= i < 3 and 0 <= j < 3
            blocks.append(turned[at : at + 64, :] if inside else none)
        return across(blocks)

    for d in range(4):
        for k, column in enumerate((0, 1, 2, -1)):
            ws_ref[d, 64 * k : 64 * k + 64, :] = line(d, column)
    for t in range(2):
        for k in range(4):
            wb_ref[t, 64 * k : 64 * k + 64, :] = line(2 * t + k // 2, k % 2)
    for t, column in ((2, 2), (3, -1)):
        for d in range(4):
            wb_ref[t, 64 * d : 64 * d + 64, :] = line(d, column)
    ratio = wpro[...].astype(F32) * (spro[...] / sexp[...])
    high = ratio.astype(BF16)
    rest = (ratio - high.astype(F32)).astype(BF16)
    blank = jnp.zeros((64, 256), BF16)
    for n in range(2):
        wo_ref[n, 0:64, :] = wexp[...] if n == 0 else blank
        wo_ref[n, 64:128, :] = blank if n == 0 else wexp[...]
        wo_ref[n, 128:192, :] = high
        wo_ref[n, 192:256, :] = rest
    shift = hexp[...] + hpro[...]
    vec_ref[0:1, :] = across([sred[...]] * 4)
    vec_ref[1:2, :] = across([hred[...]] * 4)
    vec_ref[2:3, :] = across([sspa[...]] * 4)
    vec_ref[3:4, :] = across([hspa[...]] * 4)
    vec_ref[4:5, :] = -shift / sexp[...]
    vec_ref[5:6, :] = sexp[...] * (1.0 / positions)
    vec_ref[6:7, :] = shift


def block_kernel(devices, nt, *refs):
    tiles_ref = refs[0]
    flat = refs[1:15]
    feat_ref, mean_ref = refs[15:17]
    held = refs[17:31]
    x_ref, wr_ref, ws_ref, wb_ref, wo_ref, vec_ref = refs[31:37]
    red_ref, spa_ref, mcol_ref, member_ref = refs[37:41]
    pooled_ref = refs[47]
    part_ref, land_ref, tile_sem, flat_sem, send_sem, recv_sem = refs[41:47]
    slots, side, width = tiles_ref.shape
    steps = slots // nt
    pairs = width // 128
    rows = nt * side
    half = rows // 2
    me = lax.axis_index("row")
    barrier = pltpu.get_barrier_semaphore()

    def peer(turn):
        return lax.rem(me + turn, devices)

    def tile_copy(step):
        at = pl.ds(pl.multiple_of(step * nt, nt), nt)
        return pltpu.make_async_copy(tiles_ref.at[at], x_ref.at[at], tile_sem.at[step])

    copies = [
        pltpu.make_async_copy(flat[n], held[n], flat_sem.at[n]) for n in range(len(flat))
    ]
    for copy in copies[2:]:
        copy.start()
    tile_copy(0).start()
    for copy in copies[:2]:
        copy.start()
    tile_copy(1).start()

    def greet(turn, carry):
        pl.semaphore_signal(
            barrier, inc=1, device_id={"row": peer(turn)}, device_id_type=pl.DeviceIdType.MESH
        )
        return carry

    lax.fori_loop(1, devices, greet, 0)
    for copy in copies:
        copy.wait()
    mask_ref, ids_ref = held[0:2]
    prepare(held[2:], wr_ref, ws_ref, wb_ref, wo_ref, vec_ref, side * side)
    row = lax.broadcasted_iota(jnp.int32, (slots, slots), 0)
    col = lax.broadcasted_iota(jnp.int32, (slots, slots), 1)
    diag = jnp.where(row == col, mask_ref[...].astype(F32), 0.0).astype(BF16)
    mcol_ref[...] = jnp.dot(diag, jnp.ones((slots, 128), BF16), preferred_element_type=F32)
    row = lax.broadcasted_iota(jnp.int32, (8 * devices, slots), 0)
    region = row // 8 * 4 + row % 4
    member = jnp.where(region == ids_ref[...], 1.0, 0.0).astype(BF16)
    member_ref[...] = member
    counts = jnp.dot(member, mcol_ref[...].astype(BF16), preferred_element_type=F32)
    place = lax.broadcasted_iota(jnp.int32, (8 * devices, 128), 0) % 8
    lane = lax.broadcasted_iota(jnp.int32, (8 * devices, 128), 1)
    counts = jnp.where(place == lane, counts, 0.0).reshape(devices, 8, 128)
    part_ref[:, 8:9, :] = jnp.sum(counts, axis=1, keepdims=True)

    scale_r, shift_r = vec_ref[0:1, :], vec_ref[1:2, :]
    scale_s, shift_s = vec_ref[2:3, :], vec_ref[3:4, :]
    floor, scale_o, shift_o = vec_ref[4:5, :], vec_ref[5:6, :], vec_ref[6:7, :]

    def block(step, carry):
        tile_copy(step).wait()

        @pl.when(step + 2 < steps)
        def _():
            tile_copy(step + 2).start()

        at = pl.ds(pl.multiple_of(step * nt, nt), nt)
        x = x_ref[at].reshape(rows, width)
        for g in range(pairs // 2):
            r = jnp.dot(x[:, 256 * g : 256 * g + 256], wr_ref[...], preferred_element_type=F32)
            r = jnp.maximum(r * scale_r + shift_r, 0.0)
            for h in range(2):
                red_ref[2 * g + h, :, 8 : 8 + side, :] = r[:, 128 * h : 128 * h + 128].reshape(
                    nt, side, 128
                )

        low = lax.broadcasted_iota(jnp.int32, (half, 128), 1) < 64
        tall = [
            [
                red_ref[p, :, pl.ds(7 + d, 8, stride=2), :].reshape(half, 128).astype(BF16)
                for d in range(4)
            ]
            for p in range(pairs)
        ]
        def swap(v):
            return across([v[:, 64:128], v[:, 0:64]])

        def side_of(p, d):
            if p == 0:
                return jnp.where(low, tall[1][d], swap(tall[1][d + 1]))
            return jnp.where(low, swap(tall[p - 1][d]), tall[p - 1][d + 1])

        for p in range(pairs):
            if 0 < p < pairs - 1:
                lhs = [
                    across([tall[p][d], jnp.where(low, tall[p + 1][d], tall[p - 1][d])])
                    for d in range(4)
                ]
                weights = [ws_ref[d] for d in range(4)]
            else:
                lhs = [across([tall[p][d], tall[p][d + 1]]) for d in (0, 2)]
                lhs.append(across([side_of(p, 0), side_of(p, 2)]))
                weights = [wb_ref[0], wb_ref[1], wb_ref[2 + int(p > 0)]]
            acc = None
            for v, w in zip(lhs, weights):
                term = jnp.dot(v, w, preferred_element_type=F32)
                acc = term if acc is None else acc + term
            s = jnp.maximum(acc * scale_s + shift_s, 0.0)
            spa_ref[p, pl.ds(0, half, stride=2), :] = s[:, 0:128]
            spa_ref[p, pl.ds(1, half, stride=2), :] = s[:, 128:256]

        group = 8
        deep = group * side
        low = lax.broadcasted_iota(jnp.int32, (deep, 128), 1) < 64
        for part in range(nt // group):
            r = slice(deep * part, deep * part + deep)
            first, second = [], []
            for p in range(pairs):
                xp = x[r, 128 * p : 128 * p + 128]
                xr = across([xp[:, 64:128], xp[:, 0:64]])
                sp = spa_ref[p, r, :].astype(BF16)
                first.append(across([sp, jnp.where(low, xp, xr)]))
                second.append(across([sp, jnp.where(low, xr, xp)]))
            z0 = jnp.dot(
                jnp.concatenate(first, axis=0), wo_ref[0], preferred_element_type=F32
            )
            z1 = jnp.dot(
                jnp.concatenate(second, axis=0), wo_ref[1], preferred_element_type=F32
            )
            total = None
            for p in range(pairs):
                q = slice(deep * p, deep * p + deep)
                z = jnp.maximum(z0[q], floor) + jnp.maximum(z1[q], floor)
                total = z if total is None else total + z
            pooled = jnp.sum(total.reshape(group, side, 256), axis=1)
            pooled_ref[group * part : group * part + group, :] = pooled
        keep = mcol_ref[at, :]
        pooled = (pooled_ref[...] * scale_o + shift_o) * across([keep, keep])
        feat_ref[at, :] = pooled.astype(BF16)
        return carry

    red_ref[:, :, 0:8, :] = jnp.zeros((pairs, nt, 8, 128), F32)
    red_ref[:, :, 24:32, :] = jnp.zeros((pairs, nt, 8, 128), F32)
    lax.fori_loop(0, steps, block, 0)

    sums = jnp.dot(member_ref[...], feat_ref[...], preferred_element_type=F32)
    sums = jnp.where(place < 4, sums[:, 0:128], sums[:, 128:256])
    part_ref[:, 0:8, :] = sums.reshape(devices, 8, 128)
    pl.semaphore_wait(barrier, devices - 1)

    def send(turn, carry):
        pltpu.make_async_remote_copy(
            src_ref=part_ref.at[peer(turn)],
            dst_ref=land_ref.at[turn],
            send_sem=send_sem,
            recv_sem=recv_sem,
            device_id={"row": peer(turn)},
            device_id_type=pl.DeviceIdType.MESH,
        ).start()
        return carry

    lax.fori_loop(1, devices, send, 0)
    land_ref[0] = part_ref[me]
    others = land_ref.at[pl.ds(1, devices - 1)]
    pltpu.make_async_copy(others, others, recv_sem).wait()
    landed = jnp.sum(land_ref[...], axis=0)
    row = lax.broadcasted_iota(jnp.int32, (8, 128), 0) % 4
    lane = lax.broadcasted_iota(jnp.int32, (8, 128), 1)
    count = jnp.sum(jnp.where(row == lane, landed[8:9], 0.0), axis=1, keepdims=True)
    means = landed[0:8] / jnp.maximum(count, 1.0)
    mean_ref[:, 0:128] = means[0:4]
    mean_ref[:, 128:256] = means[4:8]
    sent = part_ref.at[pl.ds(1, devices - 1)]
    pltpu.make_async_copy(sent, sent, send_sem).wait()


def write_kernel(feat_ref, mean_ref, feat_out, mean_out, sem):
    copies = [
        pltpu.make_async_copy(feat_ref, feat_out, sem.at[0]),
        pltpu.make_async_copy(mean_ref, mean_out, sem.at[1]),
    ]
    for copy in copies:
        copy.start()
    for copy in copies:
        copy.wait()


def body(tiles, tile_mask, region_ids, *params, devices):
    slots, side, width = tiles.shape
    c_out = params[6].shape[1]
    nt = pick_block(slots)
    pairs = width // 128
    flat = [p if p.ndim == 2 else p.reshape(1, -1) for p in params]
    flat[3] = params[3].T
    flat = [tile_mask.reshape(1, slots), region_ids.reshape(1, slots)] + flat
    feat, mean = pl.pallas_call(
        functools.partial(block_kernel, devices, nt),
        in_specs=[pl.BlockSpec(memory_space=pltpu.HBM)] * (1 + len(flat)),
        out_specs=[pl.BlockSpec(memory_space=pltpu.VMEM)] * 2,
        out_shape=[pltpu.VMEM((slots, c_out), BF16), pltpu.VMEM((4, c_out), F32)],
        scratch_shapes=[pltpu.VMEM(p.shape, p.dtype) for p in flat]
        + [
            pltpu.VMEM((slots, side, width), BF16),
            pltpu.VMEM((256, 256), BF16),
            pltpu.VMEM((4, 256, 256), BF16),
            pltpu.VMEM((4, 256, 256), BF16),
            pltpu.VMEM((2, 256, 256), BF16),
            pltpu.VMEM((8, 256), F32),
            pltpu.VMEM((pairs, nt, side + 16, 128), F32),
            pltpu.VMEM((pairs, nt * side, 128), F32),
            pltpu.VMEM((slots, 128), F32),
            pltpu.VMEM((8 * devices, slots), BF16),
            pltpu.VMEM((devices, 9, 128), F32),
            pltpu.VMEM((devices, 9, 128), F32),
            pltpu.SemaphoreType.DMA((slots // nt,)),
            pltpu.SemaphoreType.DMA((len(flat),)),
            pltpu.SemaphoreType.DMA,
            pltpu.SemaphoreType.DMA,
            pltpu.VMEM((nt, 256), F32),
        ],
        compiler_params=pltpu.CompilerParams(
            vmem_limit_bytes=VMEM_LIMIT, collective_id=0, has_side_effects=True
        ),
        name="block_features",
    )(tiles, *flat)
    return pl.pallas_call(
        write_kernel,
        in_specs=[pl.BlockSpec(memory_space=pltpu.VMEM)] * 2,
        out_specs=[pl.BlockSpec(memory_space=pltpu.HBM)] * 2,
        out_shape=[
            jax.ShapeDtypeStruct((slots, c_out), BF16),
            jax.ShapeDtypeStruct((4, c_out), F32),
        ],
        scratch_shapes=[pltpu.SemaphoreType.DMA((2,))],
        name="write_out",
    )(
        pltpu.with_memory_space_constraint(feat, pltpu.VMEM),
        pltpu.with_memory_space_constraint(mean, pltpu.VMEM),
    )


def solution(mesh):
    devices = mesh.shape["row"]
    split = P(("slides", "row"))
    return jax.shard_map(
        functools.partial(body, devices=devices),
        mesh=mesh,
        in_specs=(P(("slides", "row"), None, None), split, split) + (P(),) * 12,
        out_specs=(P(("slides", "row"), None), P(("slides", "row"), None)),
        check_vma=False,
    )
```

```python
import functools

import jax
import jax.numpy as jnp
from jax import lax
from jax.experimental import pallas as pl
from jax.experimental.pallas import tpu as pltpu
from jax.sharding import PartitionSpec as P

BLOCK = 56
VMEM_LIMIT = 58 * 1024 * 1024
F32 = jnp.float32
BF16 = jnp.bfloat16


def pick_block(slots):
    for size in (BLOCK, 32, 16):
        if slots % size == 0:
            return size
    return slots


def across(blocks):
    return jnp.concatenate(blocks, axis=1)


def prepare(raw, wr_ref, ws_ref, wb_ref, wo_ref, vec_ref, positions):
    wred, sred, hred, wspa, sspa, hspa, wexp, sexp, hexp, wpro, spro, hpro = raw
    none = jnp.zeros((64, 64), BF16)
    w = wred[...]
    for i in range(4):
        wr_ref[64 * i : 64 * i + 64, :] = across([w if i == j else none for j in range(4)])
    turned = wspa[...].T

    def line(d, column):
        blocks = []
        for n in range(4):
            i, j = d - n // 2, column - n % 2 + 1
            at = 64 * (3 * i + j)
            inside = 0 <= i < 3 and 0 <= j < 3
            blocks.append(turned[at : at + 64, :] if inside else none)
        return across(blocks)

    for d in range(4):
        for k, column in enumerate((0, 1, 2, -1)):
            ws_ref[d, 64 * k : 64 * k + 64, :] = line(d, column)
    for t in range(2):
        for k in range(4):
            wb_ref[t, 64 * k : 64 * k + 64, :] = line(2 * t + k // 2, k % 2)
    for t, column in ((2, 2), (3, -1)):
        for d in range(4):
            wb_ref[t, 64 * d : 64 * d + 64, :] = line(d, column)
    ratio = wpro[...].astype(F32) * (spro[...] / sexp[...])
    high = ratio.astype(BF16)
    rest = (ratio - high.astype(F32)).astype(BF16)
    blank = jnp.zeros((64, 256), BF16)
    for n in range(2):
        wo_ref[n, 0:64, :] = wexp[...] if n == 0 else blank
        wo_ref[n, 64:128, :] = blank if n == 0 else wexp[...]
        wo_ref[n, 128:192, :] = high
        wo_ref[n, 192:256, :] = rest
    shift = hexp[...] + hpro[...]
    vec_ref[0:1, :] = across([sred[...]] * 4)
    vec_ref[1:2, :] = across([hred[...]] * 4)
    vec_ref[2:3, :] = across([sspa[...]] * 4)
    vec_ref[3:4, :] = across([hspa[...]] * 4)
    vec_ref[4:5, :] = -shift / sexp[...]
    vec_ref[5:6, :] = sexp[...] * (1.0 / positions)
    vec_ref[6:7, :] = shift


def block_kernel(devices, nt, *refs):
    tiles_ref = refs[0]
    flat = refs[1:15]
    feat_ref, mean_ref = refs[15:17]
    held = refs[17:31]
    x_ref, wr_ref, ws_ref, wb_ref, wo_ref, vec_ref = refs[31:37]
    red_ref, spa_ref, mcol_ref, member_ref = refs[37:41]
    pooled_ref = refs[47]
    part_ref, land_ref, tile_sem, flat_sem, send_sem, recv_sem = refs[41:47]
    slots, side, width = tiles_ref.shape
    steps = slots // nt
    pairs = width // 128
    rows = nt * side
    half = rows // 2
    me = lax.axis_index("row")
    barrier = pltpu.get_barrier_semaphore()

    def peer(turn):
        return lax.rem(me + turn, devices)

    def tile_copy(step):
        at = pl.ds(pl.multiple_of(step * nt, nt), nt)
        return pltpu.make_async_copy(tiles_ref.at[at], x_ref.at[at], tile_sem.at[step])

    copies = [
        pltpu.make_async_copy(flat[n], held[n], flat_sem.at[n]) for n in range(len(flat))
    ]
    for copy in copies[2:]:
        copy.start()
    tile_copy(0).start()
    for copy in copies[:2]:
        copy.start()
    tile_copy(1).start()

    def greet(turn, carry):
        pl.semaphore_signal(
            barrier, inc=1, device_id={"row": peer(turn)}, device_id_type=pl.DeviceIdType.MESH
        )
        return carry

    lax.fori_loop(1, devices, greet, 0)
    for copy in copies:
        copy.wait()
    mask_ref, ids_ref = held[0:2]
    prepare(held[2:], wr_ref, ws_ref, wb_ref, wo_ref, vec_ref, side * side)
    row = lax.broadcasted_iota(jnp.int32, (slots, slots), 0)
    col = lax.broadcasted_iota(jnp.int32, (slots, slots), 1)
    diag = jnp.where(row == col, mask_ref[...].astype(F32), 0.0).astype(BF16)
    mcol_ref[...] = jnp.dot(diag, jnp.ones((slots, 128), BF16), preferred_element_type=F32)
    row = lax.broadcasted_iota(jnp.int32, (8 * devices, slots), 0)
    region = row // 8 * 4 + row % 4
    member = jnp.where(region == ids_ref[...], 1.0, 0.0).astype(BF16)
    member_ref[...] = member
    counts = jnp.dot(member, mcol_ref[...].astype(BF16), preferred_element_type=F32)
    place = lax.broadcasted_iota(jnp.int32, (8 * devices, 128), 0) % 8
    lane = lax.broadcasted_iota(jnp.int32, (8 * devices, 128), 1)
    counts = jnp.where(place == lane, counts, 0.0).reshape(devices, 8, 128)
    part_ref[:, 8:9, :] = jnp.sum(counts, axis=1, keepdims=True)

    scale_r, shift_r = vec_ref[0:1, :], vec_ref[1:2, :]
    scale_s, shift_s = vec_ref[2:3, :], vec_ref[3:4, :]
    floor, scale_o, shift_o = vec_ref[4:5, :], vec_ref[5:6, :], vec_ref[6:7, :]

    def block(step, carry):
        tile_copy(step).wait()

        @pl.when(step + 2 < steps)
        def _():
            tile_copy(step + 2).start()

        at = pl.ds(pl.multiple_of(step * nt, nt), nt)
        x = x_ref[at].reshape(rows, width)
        for g in range(pairs // 2):
            r = jnp.dot(x[:, 256 * g : 256 * g + 256], wr_ref[...], preferred_element_type=F32)
            r = jnp.maximum(r * scale_r + shift_r, 0.0)
            for h in range(2):
                red_ref[2 * g + h, :, 8 : 8 + side, :] = r[:, 128 * h : 128 * h + 128].reshape(
                    nt, side, 128
                )

        low = lax.broadcasted_iota(jnp.int32, (half, 128), 1) < 64
        tall = [
            [
                red_ref[p, :, pl.ds(7 + d, 8, stride=2), :].reshape(half, 128).astype(BF16)
                for d in range(4)
            ]
            for p in range(pairs)
        ]
        def swap(v):
            return across([v[:, 64:128], v[:, 0:64]])

        def side_of(p, d):
            if p == 0:
                return jnp.where(low, tall[1][d], swap(tall[1][d + 1]))
            return jnp.where(low, swap(tall[p - 1][d]), tall[p - 1][d + 1])

        for p in range(pairs):
            if 0 < p < pairs - 1:
                lhs = [
                    across([tall[p][d], jnp.where(low, tall[p + 1][d], tall[p - 1][d])])
                    for d in range(4)
                ]
                weights = [ws_ref[d] for d in range(4)]
            else:
                lhs = [across([tall[p][d], tall[p][d + 1]]) for d in (0, 2)]
                lhs.append(across([side_of(p, 0), side_of(p, 2)]))
                weights = [wb_ref[0], wb_ref[1], wb_ref[2 + int(p > 0)]]
            acc = None
            for v, w in zip(lhs, weights):
                term = jnp.dot(v, w, preferred_element_type=F32)
                acc = term if acc is None else acc + term
            s = jnp.maximum(acc * scale_s + shift_s, 0.0)
            spa_ref[p, pl.ds(0, half, stride=2), :] = s[:, 0:128]
            spa_ref[p, pl.ds(1, half, stride=2), :] = s[:, 128:256]

        group = 8
        deep = group * side
        low = lax.broadcasted_iota(jnp.int32, (deep, 128), 1) < 64
        for part in range(nt // group):
            r = slice(deep * part, deep * part + deep)
            first, second = [], []
            for p in range(pairs):
                xp = x[r, 128 * p : 128 * p + 128]
                xr = across([xp[:, 64:128], xp[:, 0:64]])
                sp = spa_ref[p, r, :].astype(BF16)
                first.append(across([sp, jnp.where(low, xp, xr)]))
                second.append(across([sp, jnp.where(low, xr, xp)]))
            z0 = jnp.dot(
                jnp.concatenate(first, axis=0), wo_ref[0], preferred_element_type=F32
            )
            z1 = jnp.dot(
                jnp.concatenate(second, axis=0), wo_ref[1], preferred_element_type=F32
            )
            total = None
            for p in range(pairs):
                q = slice(deep * p, deep * p + deep)
                z = jnp.maximum(z0[q], floor) + jnp.maximum(z1[q], floor)
                total = z if total is None else total + z
            pooled = jnp.sum(total.reshape(group, side, 256), axis=1)
            to = pl.multiple_of(step * nt + group * part, group)
            pooled_ref[pl.ds(to, group), :] = pooled
        return carry

    red_ref[:, :, 0:8, :] = jnp.zeros((pairs, nt, 8, 128), F32)
    red_ref[:, :, 24:32, :] = jnp.zeros((pairs, nt, 8, 128), F32)
    lax.fori_loop(0, steps, block, 0)
    keep = mcol_ref[...]
    pooled = (pooled_ref[...] * scale_o + shift_o) * across([keep, keep])
    feat_ref[...] = pooled.astype(BF16)

    sums = jnp.dot(member_ref[...], feat_ref[...], preferred_element_type=F32)
    sums = jnp.where(place < 4, sums[:, 0:128], sums[:, 128:256])
    part_ref[:, 0:8, :] = sums.reshape(devices, 8, 128)
    pl.semaphore_wait(barrier, devices - 1)

    def send(turn, carry):
        pltpu.make_async_remote_copy(
            src_ref=part_ref.at[peer(turn)],
            dst_ref=land_ref.at[turn],
            send_sem=send_sem,
            recv_sem=recv_sem,
            device_id={"row": peer(turn)},
            device_id_type=pl.DeviceIdType.MESH,
        ).start()
        return carry

    lax.fori_loop(1, devices, send, 0, unroll=3)
    land_ref[0] = part_ref[me]
    others = land_ref.at[pl.ds(1, devices - 1)]
    pltpu.make_async_copy(others, others, recv_sem).wait()
    landed = jnp.sum(land_ref[...], axis=0)
    row = lax.broadcasted_iota(jnp.int32, (8, 128), 0) % 4
    lane = lax.broadcasted_iota(jnp.int32, (8, 128), 1)
    count = jnp.sum(jnp.where(row == lane, landed[8:9], 0.0), axis=1, keepdims=True)
    means = landed[0:8] / jnp.maximum(count, 1.0)
    mean_ref[:, 0:128] = means[0:4]
    mean_ref[:, 128:256] = means[4:8]
    sent = part_ref.at[pl.ds(1, devices - 1)]
    pltpu.make_async_copy(sent, sent, send_sem).wait()


def write_kernel(feat_ref, mean_ref, feat_out, mean_out, sem):
    copies = [
        pltpu.make_async_copy(feat_ref, feat_out, sem.at[0]),
        pltpu.make_async_copy(mean_ref, mean_out, sem.at[1]),
    ]
    for copy in copies:
        copy.start()
    for copy in copies:
        copy.wait()


def body(tiles, tile_mask, region_ids, *params, devices):
    slots, side, width = tiles.shape
    c_out = params[6].shape[1]
    nt = pick_block(slots)
    pairs = width // 128
    flat = [p if p.ndim == 2 else p.reshape(1, -1) for p in params]
    flat[3] = params[3].T
    flat = [tile_mask.reshape(1, slots), region_ids.reshape(1, slots)] + flat
    feat, mean = pl.pallas_call(
        functools.partial(block_kernel, devices, nt),
        in_specs=[pl.BlockSpec(memory_space=pltpu.HBM)] * (1 + len(flat)),
        out_specs=[pl.BlockSpec(memory_space=pltpu.VMEM)] * 2,
        out_shape=[pltpu.VMEM((slots, c_out), BF16), pltpu.VMEM((4, c_out), F32)],
        scratch_shapes=[pltpu.VMEM(p.shape, p.dtype) for p in flat]
        + [
            pltpu.VMEM((slots, side, width), BF16),
            pltpu.VMEM((256, 256), BF16),
            pltpu.VMEM((4, 256, 256), BF16),
            pltpu.VMEM((4, 256, 256), BF16),
            pltpu.VMEM((2, 256, 256), BF16),
            pltpu.VMEM((8, 256), F32),
            pltpu.VMEM((pairs, nt, side + 16, 128), F32),
            pltpu.VMEM((pairs, nt * side, 128), F32),
            pltpu.VMEM((slots, 128), F32),
            pltpu.VMEM((8 * devices, slots), BF16),
            pltpu.VMEM((devices, 9, 128), F32),
            pltpu.VMEM((devices, 9, 128), F32),
            pltpu.SemaphoreType.DMA((slots // nt,)),
            pltpu.SemaphoreType.DMA((len(flat),)),
            pltpu.SemaphoreType.DMA,
            pltpu.SemaphoreType.DMA,
            pltpu.VMEM((slots, 256), F32),
        ],
        compiler_params=pltpu.CompilerParams(
            vmem_limit_bytes=VMEM_LIMIT, collective_id=0, has_side_effects=True
        ),
        name="block_features",
    )(tiles, *flat)
    return pl.pallas_call(
        write_kernel,
        in_specs=[pl.BlockSpec(memory_space=pltpu.VMEM)] * 2,
        out_specs=[pl.BlockSpec(memory_space=pltpu.HBM)] * 2,
        out_shape=[
            jax.ShapeDtypeStruct((slots, c_out), BF16),
            jax.ShapeDtypeStruct((4, c_out), F32),
        ],
        scratch_shapes=[pltpu.SemaphoreType.DMA((2,))],
        name="write_out",
    )(
        pltpu.with_memory_space_constraint(feat, pltpu.VMEM),
        pltpu.with_memory_space_constraint(mean, pltpu.VMEM),
    )


def solution(mesh):
    devices = mesh.shape["row"]
    split = P(("slides", "row"))
    return jax.shard_map(
        functools.partial(body, devices=devices),
        mesh=mesh,
        in_specs=(P(("slides", "row"), None, None), split, split) + (P(),) * 12,
        out_specs=(P(("slides", "row"), None), P(("slides", "row"), None)),
        check_vma=False,
    )
```

```python
import functools

import jax
import jax.numpy as jnp
from jax import lax
from jax.experimental import pallas as pl
from jax.experimental.pallas import tpu as pltpu
from jax.sharding import PartitionSpec as P

BLOCK = 56
VMEM_LIMIT = 58 * 1024 * 1024
F32 = jnp.float32
BF16 = jnp.bfloat16


def pick_block(slots):
    for size in (BLOCK, 32, 16):
        if slots % size == 0:
            return size
    return slots


def across(blocks):
    return jnp.concatenate(blocks, axis=1)


def prepare(raw, wr_ref, ws_ref, wb_ref, wo_ref, vec_ref, positions):
    wred, sred, hred, wspa, sspa, hspa, wexp, sexp, hexp, wpro, spro, hpro = raw
    none = jnp.zeros((64, 64), BF16)
    w = wred[...]
    for i in range(4):
        wr_ref[64 * i : 64 * i + 64, :] = across([w if i == j else none for j in range(4)])
    turned = wspa[...].T

    def line(d, column):
        blocks = []
        for n in range(4):
            i, j = d - n // 2, column - n % 2 + 1
            at = 64 * (3 * i + j)
            inside = 0 <= i < 3 and 0 <= j < 3
            blocks.append(turned[at : at + 64, :] if inside else none)
        return across(blocks)

    for d in range(4):
        for k, column in enumerate((0, 1, 2, -1)):
            ws_ref[d, 64 * k : 64 * k + 64, :] = line(d, column)
    for t in range(2):
        for k in range(4):
            wb_ref[t, 64 * k : 64 * k + 64, :] = line(2 * t + k // 2, k % 2)
    for t, column in ((2, 2), (3, -1)):
        for d in range(4):
            wb_ref[t, 64 * d : 64 * d + 64, :] = line(d, column)
    ratio = wpro[...].astype(F32) * (spro[...] / sexp[...])
    high = ratio.astype(BF16)
    rest = (ratio - high.astype(F32)).astype(BF16)
    blank = jnp.zeros((64, 256), BF16)
    for n in range(2):
        wo_ref[n, 0:64, :] = wexp[...] if n == 0 else blank
        wo_ref[n, 64:128, :] = blank if n == 0 else wexp[...]
        wo_ref[n, 128:192, :] = high
        wo_ref[n, 192:256, :] = rest
    shift = hexp[...] + hpro[...]
    vec_ref[0:1, :] = across([sred[...]] * 4)
    vec_ref[1:2, :] = across([hred[...]] * 4)
    vec_ref[2:3, :] = across([sspa[...]] * 4)
    vec_ref[3:4, :] = across([hspa[...]] * 4)
    vec_ref[4:5, :] = -shift / sexp[...]
    vec_ref[5:6, :] = sexp[...] * (1.0 / positions)
    vec_ref[6:7, :] = shift


def block_kernel(devices, nt, *refs):
    tiles_ref = refs[0]
    flat = refs[1:15]
    feat_ref, mean_ref = refs[15:17]
    held = refs[17:31]
    x_ref, wr_ref, ws_ref, wb_ref, wo_ref, vec_ref = refs[31:37]
    red_ref, spa_ref, mcol_ref, member_ref = refs[37:41]
    pooled_ref = refs[47]
    part_ref, land_ref, tile_sem, flat_sem, send_sem, recv_sem = refs[41:47]
    slots, side, width = tiles_ref.shape
    steps = slots // nt
    pairs = width // 128
    rows = nt * side
    half = rows // 2
    me = lax.axis_index("row")
    barrier = pltpu.get_barrier_semaphore()

    def peer(turn):
        return lax.rem(me + turn, devices)

    def tile_copy(step):
        at = pl.ds(pl.multiple_of(step * nt, nt), nt)
        return pltpu.make_async_copy(tiles_ref.at[at], x_ref.at[at], tile_sem.at[step])

    copies = [
        pltpu.make_async_copy(flat[n], held[n], flat_sem.at[n]) for n in range(len(flat))
    ]
    tile_copy(0).start()
    for copy in copies:
        copy.start()
    tile_copy(1).start()

    def greet(turn, carry):
        pl.semaphore_signal(
            barrier, inc=1, device_id={"row": peer(turn)}, device_id_type=pl.DeviceIdType.MESH
        )
        return carry

    lax.fori_loop(1, devices, greet, 0)
    for copy in copies:
        copy.wait()
    mask_ref, ids_ref = held[0:2]
    prepare(held[2:], wr_ref, ws_ref, wb_ref, wo_ref, vec_ref, side * side)
    row = lax.broadcasted_iota(jnp.int32, (slots, slots), 0)
    col = lax.broadcasted_iota(jnp.int32, (slots, slots), 1)
    diag = jnp.where(row == col, mask_ref[...].astype(F32), 0.0).astype(BF16)
    mcol_ref[...] = jnp.dot(diag, jnp.ones((slots, 128), BF16), preferred_element_type=F32)
    row = lax.broadcasted_iota(jnp.int32, (8 * devices, slots), 0)
    region = row // 8 * 4 + row % 4
    member = jnp.where(region == ids_ref[...], 1.0, 0.0).astype(BF16)
    member_ref[...] = member
    counts = jnp.dot(member, mcol_ref[...].astype(BF16), preferred_element_type=F32)
    place = lax.broadcasted_iota(jnp.int32, (8 * devices, 128), 0) % 8
    lane = lax.broadcasted_iota(jnp.int32, (8 * devices, 128), 1)
    counts = jnp.where(place == lane, counts, 0.0).reshape(devices, 8, 128)
    part_ref[:, 8:9, :] = jnp.sum(counts, axis=1, keepdims=True)

    scale_r, shift_r = vec_ref[0:1, :], vec_ref[1:2, :]
    scale_s, shift_s = vec_ref[2:3, :], vec_ref[3:4, :]
    floor, scale_o, shift_o = vec_ref[4:5, :], vec_ref[5:6, :], vec_ref[6:7, :]

    def block(step, carry):
        tile_copy(step).wait()

        @pl.when(step + 2 < steps)
        def _():
            tile_copy(step + 2).start()

        at = pl.ds(pl.multiple_of(step * nt, nt), nt)
        x = x_ref[at].reshape(rows, width)
        for g in range(pairs // 2):
            r = jnp.dot(x[:, 256 * g : 256 * g + 256], wr_ref[...], preferred_element_type=F32)
            r = jnp.maximum(r * scale_r + shift_r, 0.0)
            for h in range(2):
                red_ref[2 * g + h, :, 8 : 8 + side, :] = r[:, 128 * h : 128 * h + 128].reshape(
                    nt, side, 128
                )

        low = lax.broadcasted_iota(jnp.int32, (half, 128), 1) < 64
        tall = [
            [
                red_ref[p, :, pl.ds(7 + d, 8, stride=2), :].reshape(half, 128).astype(BF16)
                for d in range(4)
            ]
            for p in range(pairs)
        ]
        def swap(v):
            return across([v[:, 64:128], v[:, 0:64]])

        def side_of(p, d):
            if p == 0:
                return jnp.where(low, tall[1][d], swap(tall[1][d + 1]))
            return jnp.where(low, swap(tall[p - 1][d]), tall[p - 1][d + 1])

        for p in range(pairs):
            if 0 < p < pairs - 1:
                lhs = [
                    across([tall[p][d], jnp.where(low, tall[p + 1][d], tall[p - 1][d])])
                    for d in range(4)
                ]
                weights = [ws_ref[d] for d in range(4)]
            else:
                lhs = [across([tall[p][d], tall[p][d + 1]]) for d in (0, 2)]
                lhs.append(across([side_of(p, 0), side_of(p, 2)]))
                weights = [wb_ref[0], wb_ref[1], wb_ref[2 + int(p > 0)]]
            acc = None
            for v, w in zip(lhs, weights):
                term = jnp.dot(v, w, preferred_element_type=F32)
                acc = term if acc is None else acc + term
            s = jnp.maximum(acc * scale_s + shift_s, 0.0)
            spa_ref[p, pl.ds(0, half, stride=2), :] = s[:, 0:128]
            spa_ref[p, pl.ds(1, half, stride=2), :] = s[:, 128:256]

        group = 8
        deep = group * side
        low = lax.broadcasted_iota(jnp.int32, (deep, 128), 1) < 64
        for part in range(nt // group):
            r = slice(deep * part, deep * part + deep)
            first, second = [], []
            for p in range(pairs):
                xp = x[r, 128 * p : 128 * p + 128]
                xr = across([xp[:, 64:128], xp[:, 0:64]])
                sp = spa_ref[p, r, :].astype(BF16)
                first.append(across([sp, jnp.where(low, xp, xr)]))
                second.append(across([sp, jnp.where(low, xr, xp)]))
            z0 = jnp.dot(
                jnp.concatenate(first, axis=0), wo_ref[0], preferred_element_type=F32
            )
            z1 = jnp.dot(
                jnp.concatenate(second, axis=0), wo_ref[1], preferred_element_type=F32
            )
            total = None
            for p in range(pairs):
                q = slice(deep * p, deep * p + deep)
                z = jnp.maximum(z0[q], floor) + jnp.maximum(z1[q], floor)
                total = z if total is None else total + z
            pooled = jnp.sum(total.reshape(group, side, 256), axis=1)
            to = pl.multiple_of(step * nt + group * part, group)
            pooled_ref[pl.ds(to, group), :] = pooled
        return carry

    red_ref[:, :, 0:8, :] = jnp.zeros((pairs, nt, 8, 128), F32)
    red_ref[:, :, 24:32, :] = jnp.zeros((pairs, nt, 8, 128), F32)
    lax.fori_loop(0, steps, block, 0)
    keep = mcol_ref[...]
    pooled = (pooled_ref[...] * scale_o + shift_o) * across([keep, keep])
    feat_ref[...] = pooled.astype(BF16)

    sums = jnp.dot(member_ref[...], feat_ref[...], preferred_element_type=F32)
    sums = jnp.where(place < 4, sums[:, 0:128], sums[:, 128:256])
    part_ref[:, 0:8, :] = sums.reshape(devices, 8, 128)
    pl.semaphore_wait(barrier, devices - 1)

    def send(turn, carry):
        pltpu.make_async_remote_copy(
            src_ref=part_ref.at[peer(turn)],
            dst_ref=land_ref.at[turn],
            send_sem=send_sem,
            recv_sem=recv_sem,
            device_id={"row": peer(turn)},
            device_id_type=pl.DeviceIdType.MESH,
        ).start()
        return carry

    lax.fori_loop(1, devices, send, 0, unroll=3)
    land_ref[0] = part_ref[me]
    others = land_ref.at[pl.ds(1, devices - 1)]
    pltpu.make_async_copy(others, others, recv_sem).wait()
    landed = jnp.sum(land_ref[...], axis=0)
    row = lax.broadcasted_iota(jnp.int32, (8, 128), 0) % 4
    lane = lax.broadcasted_iota(jnp.int32, (8, 128), 1)
    count = jnp.sum(jnp.where(row == lane, landed[8:9], 0.0), axis=1, keepdims=True)
    means = landed[0:8] / jnp.maximum(count, 1.0)
    mean_ref[:, 0:128] = means[0:4]
    mean_ref[:, 128:256] = means[4:8]
    sent = part_ref.at[pl.ds(1, devices - 1)]
    pltpu.make_async_copy(sent, sent, send_sem).wait()


def write_kernel(feat_ref, mean_ref, feat_out, mean_out, sem):
    copies = [
        pltpu.make_async_copy(feat_ref, feat_out, sem.at[0]),
        pltpu.make_async_copy(mean_ref, mean_out, sem.at[1]),
    ]
    for copy in copies:
        copy.start()
    for copy in copies:
        copy.wait()


def body(tiles, tile_mask, region_ids, *params, devices):
    slots, side, width = tiles.shape
    c_out = params[6].shape[1]
    nt = pick_block(slots)
    pairs = width // 128
    flat = [p if p.ndim == 2 else p.reshape(1, -1) for p in params]
    flat[3] = params[3].T
    flat = [tile_mask.reshape(1, slots), region_ids.reshape(1, slots)] + flat
    feat, mean = pl.pallas_call(
        functools.partial(block_kernel, devices, nt),
        in_specs=[pl.BlockSpec(memory_space=pltpu.HBM)] * (1 + len(flat)),
        out_specs=[pl.BlockSpec(memory_space=pltpu.VMEM)] * 2,
        out_shape=[pltpu.VMEM((slots, c_out), BF16), pltpu.VMEM((4, c_out), F32)],
        scratch_shapes=[pltpu.VMEM(p.shape, p.dtype) for p in flat]
        + [
            pltpu.VMEM((slots, side, width), BF16),
            pltpu.VMEM((256, 256), BF16),
            pltpu.VMEM((4, 256, 256), BF16),
            pltpu.VMEM((4, 256, 256), BF16),
            pltpu.VMEM((2, 256, 256), BF16),
            pltpu.VMEM((8, 256), F32),
            pltpu.VMEM((pairs, nt, side + 16, 128), F32),
            pltpu.VMEM((pairs, nt * side, 128), F32),
            pltpu.VMEM((slots, 128), F32),
            pltpu.VMEM((8 * devices, slots), BF16),
            pltpu.VMEM((devices, 9, 128), F32),
            pltpu.VMEM((devices, 9, 128), F32),
            pltpu.SemaphoreType.DMA((slots // nt,)),
            pltpu.SemaphoreType.DMA((len(flat),)),
            pltpu.SemaphoreType.DMA,
            pltpu.SemaphoreType.DMA,
            pltpu.VMEM((slots, 256), F32),
        ],
        compiler_params=pltpu.CompilerParams(
            vmem_limit_bytes=VMEM_LIMIT, collective_id=0, has_side_effects=True
        ),
        name="block_features",
    )(tiles, *flat)
    return pl.pallas_call(
        write_kernel,
        in_specs=[pl.BlockSpec(memory_space=pltpu.VMEM)] * 2,
        out_specs=[pl.BlockSpec(memory_space=pltpu.HBM)] * 2,
        out_shape=[
            jax.ShapeDtypeStruct((slots, c_out), BF16),
            jax.ShapeDtypeStruct((4, c_out), F32),
        ],
        scratch_shapes=[pltpu.SemaphoreType.DMA((2,))],
        name="write_out",
    )(
        pltpu.with_memory_space_constraint(feat, pltpu.VMEM),
        pltpu.with_memory_space_constraint(mean, pltpu.VMEM),
    )


def solution(mesh):
    devices = mesh.shape["row"]
    split = P(("slides", "row"))
    return jax.shard_map(
        functools.partial(body, devices=devices),
        mesh=mesh,
        in_specs=(P(("slides", "row"), None, None), split, split) + (P(),) * 12,
        out_specs=(P(("slides", "row"), None), P(("slides", "row"), None)),
        check_vma=False,
    )
```

```python
import functools

import jax
import jax.numpy as jnp
from jax import lax
from jax.experimental import pallas as pl
from jax.experimental.pallas import tpu as pltpu
from jax.sharding import PartitionSpec as P

BLOCK = 56
VMEM_LIMIT = 58 * 1024 * 1024
F32 = jnp.float32
BF16 = jnp.bfloat16


def pick_block(slots):
    for size in (BLOCK, 32, 16):
        if slots % size == 0:
            return size
    return slots


def across(blocks):
    return jnp.concatenate(blocks, axis=1)


def prepare(raw, wr_ref, ws_ref, wb_ref, wo_ref, vec_ref, positions):
    wred, sred, hred, wspa, sspa, hspa, wexp, sexp, hexp, wpro, spro, hpro = raw
    none = jnp.zeros((64, 64), BF16)
    w = wred[...]
    for i in range(4):
        wr_ref[64 * i : 64 * i + 64, :] = across([w if i == j else none for j in range(4)])
    turned = wspa[...].T

    def line(d, column):
        blocks = []
        for n in range(4):
            i, j = d - n // 2, column - n % 2 + 1
            at = 64 * (3 * i + j)
            inside = 0 <= i < 3 and 0 <= j < 3
            blocks.append(turned[at : at + 64, :] if inside else none)
        return across(blocks)

    for d in range(4):
        for k, column in enumerate((0, 1, 2, -1)):
            ws_ref[d, 64 * k : 64 * k + 64, :] = line(d, column)
    for t in range(2):
        for k in range(4):
            wb_ref[t, 64 * k : 64 * k + 64, :] = line(2 * t + k // 2, k % 2)
    for t, column in ((2, 2), (3, -1)):
        for d in range(4):
            wb_ref[t, 64 * d : 64 * d + 64, :] = line(d, column)
    ratio = wpro[...].astype(F32) * (spro[...] / sexp[...])
    high = ratio.astype(BF16)
    rest = (ratio - high.astype(F32)).astype(BF16)
    blank = jnp.zeros((64, 256), BF16)
    for n in range(2):
        wo_ref[n, 0:64, :] = wexp[...] if n == 0 else blank
        wo_ref[n, 64:128, :] = blank if n == 0 else wexp[...]
        wo_ref[n, 128:192, :] = high
        wo_ref[n, 192:256, :] = rest
    shift = hexp[...] + hpro[...]
    vec_ref[0:1, :] = across([sred[...]] * 4)
    vec_ref[1:2, :] = across([hred[...]] * 4)
    vec_ref[2:3, :] = across([sspa[...]] * 4)
    vec_ref[3:4, :] = across([hspa[...]] * 4)
    vec_ref[4:5, :] = -shift / sexp[...]
    vec_ref[5:6, :] = sexp[...] * (1.0 / positions)
    vec_ref[6:7, :] = shift


def block_kernel(devices, nt, *refs):
    tiles_ref = refs[0]
    flat = refs[1:15]
    feat_ref, mean_ref = refs[15:17]
    held = refs[17:31]
    x_ref, wr_ref, ws_ref, wb_ref, wo_ref, vec_ref = refs[31:37]
    red_ref, spa_ref, mcol_ref, member_ref = refs[37:41]
    pooled_ref = refs[47]
    part_ref, land_ref, tile_sem, flat_sem, send_sem, recv_sem = refs[41:47]
    slots, side, width = tiles_ref.shape
    steps = slots // nt
    pairs = width // 128
    rows = nt * side
    half = rows // 2
    me = lax.axis_index("row")
    barrier = pltpu.get_barrier_semaphore()

    def peer(turn):
        return lax.rem(me + turn, devices)

    def tile_copy(step):
        at = pl.ds(pl.multiple_of(step * nt, nt), nt)
        return pltpu.make_async_copy(tiles_ref.at[at], x_ref.at[at], tile_sem.at[step])

    copies = [
        pltpu.make_async_copy(flat[n], held[n], flat_sem.at[n]) for n in range(len(flat))
    ]
    for copy in copies[2:]:
        copy.start()
    tile_copy(0).start()
    for copy in copies[:2]:
        copy.start()
    tile_copy(1).start()

    def greet(turn, carry):
        pl.semaphore_signal(
            barrier, inc=1, device_id={"row": peer(turn)}, device_id_type=pl.DeviceIdType.MESH
        )
        return carry

    lax.fori_loop(1, devices, greet, 0)
    for copy in copies:
        copy.wait()
    mask_ref, ids_ref = held[0:2]
    prepare(held[2:], wr_ref, ws_ref, wb_ref, wo_ref, vec_ref, side * side)
    row = lax.broadcasted_iota(jnp.int32, (slots, slots), 0)
    col = lax.broadcasted_iota(jnp.int32, (slots, slots), 1)
    diag = jnp.where(row == col, mask_ref[...].astype(F32), 0.0).astype(BF16)
    mcol_ref[...] = jnp.dot(diag, jnp.ones((slots, 128), BF16), preferred_element_type=F32)
    row = lax.broadcasted_iota(jnp.int32, (8 * devices, slots), 0)
    region = row // 8 * 4 + row % 4
    member = jnp.where(region == ids_ref[...], 1.0, 0.0).astype(BF16)
    member_ref[...] = member
    counts = jnp.dot(member, mcol_ref[...].astype(BF16), preferred_element_type=F32)
    place = lax.broadcasted_iota(jnp.int32, (8 * devices, 128), 0) % 8
    lane = lax.broadcasted_iota(jnp.int32, (8 * devices, 128), 1)
    counts = jnp.where(place == lane, counts, 0.0).reshape(devices, 8, 128)
    part_ref[:, 8:9, :] = jnp.sum(counts, axis=1, keepdims=True)

    scale_r, shift_r = vec_ref[0:1, :], vec_ref[1:2, :]
    scale_s, shift_s = vec_ref[2:3, :], vec_ref[3:4, :]
    floor, scale_o, shift_o = vec_ref[4:5, :], vec_ref[5:6, :], vec_ref[6:7, :]

    def block(step, carry):
        tile_copy(step).wait()

        @pl.when(step + 2 < steps)
        def _():
            tile_copy(step + 2).start()

        at = pl.ds(pl.multiple_of(step * nt, nt), nt)
        x = x_ref[at].reshape(rows, width)
        for g in range(pairs // 2):
            r = jnp.dot(x[:, 256 * g : 256 * g + 256], wr_ref[...], preferred_element_type=F32)
            r = jnp.maximum(r * scale_r + shift_r, 0.0)
            for h in range(2):
                red_ref[2 * g + h, :, 8 : 8 + side, :] = r[:, 128 * h : 128 * h + 128].reshape(
                    nt, side, 128
                )

        low = lax.broadcasted_iota(jnp.int32, (half, 128), 1) < 64
        tall = [
            [
                red_ref[p, :, pl.ds(7 + d, 8, stride=2), :].reshape(half, 128).astype(BF16)
                for d in range(4)
            ]
            for p in range(pairs)
        ]
        def swap(v):
            return across([v[:, 64:128], v[:, 0:64]])

        def side_of(p, d):
            if p == 0:
                return jnp.where(low, tall[1][d], swap(tall[1][d + 1]))
            return jnp.where(low, swap(tall[p - 1][d]), tall[p - 1][d + 1])

        for p in range(pairs):
            if 0 < p < pairs - 1:
                lhs = [
                    across([tall[p][d], jnp.where(low, tall[p + 1][d], tall[p - 1][d])])
                    for d in range(4)
                ]
                weights = [ws_ref[d] for d in range(4)]
            else:
                lhs = [across([tall[p][d], tall[p][d + 1]]) for d in (0, 2)]
                lhs.append(across([side_of(p, 0), side_of(p, 2)]))
                weights = [wb_ref[0], wb_ref[1], wb_ref[2 + int(p > 0)]]
            acc = None
            for v, w in zip(lhs, weights):
                term = jnp.dot(v, w, preferred_element_type=F32)
                acc = term if acc is None else acc + term
            s = jnp.maximum(acc * scale_s + shift_s, 0.0)
            spa_ref[p, pl.ds(0, half, stride=2), :] = s[:, 0:128]
            spa_ref[p, pl.ds(1, half, stride=2), :] = s[:, 128:256]

        group = 8
        deep = group * side
        low = lax.broadcasted_iota(jnp.int32, (deep, 128), 1) < 64
        for part in range(nt // group):
            r = slice(deep * part, deep * part + deep)
            first, second = [], []
            for p in range(pairs):
                xp = x[r, 128 * p : 128 * p + 128]
                xr = across([xp[:, 64:128], xp[:, 0:64]])
                sp = spa_ref[p, r, :].astype(BF16)
                first.append(across([sp, jnp.where(low, xp, xr)]))
                second.append(across([sp, jnp.where(low, xr, xp)]))
            z0 = jnp.dot(
                jnp.concatenate(first, axis=0), wo_ref[0], preferred_element_type=F32
            )
            z1 = jnp.dot(
                jnp.concatenate(second, axis=0), wo_ref[1], preferred_element_type=F32
            )
            total = None
            for p in range(pairs):
                q = slice(deep * p, deep * p + deep)
                z = jnp.maximum(z0[q], floor) + jnp.maximum(z1[q], floor)
                total = z if total is None else total + z
            pooled = jnp.sum(total.reshape(group, side, 256), axis=1)
            to = pl.multiple_of(step * nt + group * part, group)
            pooled_ref[pl.ds(to, group), :] = pooled
        return carry

    red_ref[:, :, 0:8, :] = jnp.zeros((pairs, nt, 8, 128), F32)
    red_ref[:, :, 24:32, :] = jnp.zeros((pairs, nt, 8, 128), F32)
    lax.fori_loop(0, steps, block, 0)
    keep = mcol_ref[...]
    pooled = (pooled_ref[...] * scale_o + shift_o) * across([keep, keep])
    feat_ref[...] = pooled.astype(BF16)

    sums = jnp.dot(member_ref[...], feat_ref[...], preferred_element_type=F32)
    sums = jnp.where(place < 4, sums[:, 0:128], sums[:, 128:256])
    part_ref[:, 0:8, :] = sums.reshape(devices, 8, 128)
    pl.semaphore_wait(barrier, devices - 1)

    def send(count, carry):
        turn = lax.rem(count + devices - me, devices)

        @pl.when(turn > 0)
        def _():
            pltpu.make_async_remote_copy(
                src_ref=part_ref.at[peer(turn)],
                dst_ref=land_ref.at[turn],
                send_sem=send_sem,
                recv_sem=recv_sem,
                device_id={"row": peer(turn)},
                device_id_type=pl.DeviceIdType.MESH,
            ).start()

        return carry

    lax.fori_loop(0, devices, send, 0)
    land_ref[0] = part_ref[me]
    others = land_ref.at[pl.ds(1, devices - 1)]
    pltpu.make_async_copy(others, others, recv_sem).wait()
    landed = jnp.sum(land_ref[...], axis=0)
    row = lax.broadcasted_iota(jnp.int32, (8, 128), 0) % 4
    lane = lax.broadcasted_iota(jnp.int32, (8, 128), 1)
    count = jnp.sum(jnp.where(row == lane, landed[8:9], 0.0), axis=1, keepdims=True)
    means = landed[0:8] / jnp.maximum(count, 1.0)
    mean_ref[:, 0:128] = means[0:4]
    mean_ref[:, 128:256] = means[4:8]
    sent = part_ref.at[pl.ds(1, devices - 1)]
    pltpu.make_async_copy(sent, sent, send_sem).wait()


def write_kernel(feat_ref, mean_ref, feat_out, mean_out, sem):
    copies = [
        pltpu.make_async_copy(feat_ref, feat_out, sem.at[0]),
        pltpu.make_async_copy(mean_ref, mean_out, sem.at[1]),
    ]
    for copy in copies:
        copy.start()
    for copy in copies:
        copy.wait()


def body(tiles, tile_mask, region_ids, *params, devices):
    slots, side, width = tiles.shape
    c_out = params[6].shape[1]
    nt = pick_block(slots)
    pairs = width // 128
    flat = [p if p.ndim == 2 else p.reshape(1, -1) for p in params]
    flat[3] = params[3].T
    flat = [tile_mask.reshape(1, slots), region_ids.reshape(1, slots)] + flat
    feat, mean = pl.pallas_call(
        functools.partial(block_kernel, devices, nt),
        in_specs=[pl.BlockSpec(memory_space=pltpu.HBM)] * (1 + len(flat)),
        out_specs=[pl.BlockSpec(memory_space=pltpu.VMEM)] * 2,
        out_shape=[pltpu.VMEM((slots, c_out), BF16), pltpu.VMEM((4, c_out), F32)],
        scratch_shapes=[pltpu.VMEM(p.shape, p.dtype) for p in flat]
        + [
            pltpu.VMEM((slots, side, width), BF16),
            pltpu.VMEM((256, 256), BF16),
            pltpu.VMEM((4, 256, 256), BF16),
            pltpu.VMEM((4, 256, 256), BF16),
            pltpu.VMEM((2, 256, 256), BF16),
            pltpu.VMEM((8, 256), F32),
            pltpu.VMEM((pairs, nt, side + 16, 128), F32),
            pltpu.VMEM((pairs, nt * side, 128), F32),
            pltpu.VMEM((slots, 128), F32),
            pltpu.VMEM((8 * devices, slots), BF16),
            pltpu.VMEM((devices, 9, 128), F32),
            pltpu.VMEM((devices, 9, 128), F32),
            pltpu.SemaphoreType.DMA((slots // nt,)),
            pltpu.SemaphoreType.DMA((len(flat),)),
            pltpu.SemaphoreType.DMA,
            pltpu.SemaphoreType.DMA,
            pltpu.VMEM((slots, 256), F32),
        ],
        compiler_params=pltpu.CompilerParams(
            vmem_limit_bytes=VMEM_LIMIT, collective_id=0, has_side_effects=True
        ),
        name="block_features",
    )(tiles, *flat)
    return pl.pallas_call(
        write_kernel,
        in_specs=[pl.BlockSpec(memory_space=pltpu.VMEM)] * 2,
        out_specs=[pl.BlockSpec(memory_space=pltpu.HBM)] * 2,
        out_shape=[
            jax.ShapeDtypeStruct((slots, c_out), BF16),
            jax.ShapeDtypeStruct((4, c_out), F32),
        ],
        scratch_shapes=[pltpu.SemaphoreType.DMA((2,))],
        name="write_out",
    )(
        pltpu.with_memory_space_constraint(feat, pltpu.VMEM),
        pltpu.with_memory_space_constraint(mean, pltpu.VMEM),
    )


def solution(mesh):
    devices = mesh.shape["row"]
    split = P(("slides", "row"))
    return jax.shard_map(
        functools.partial(body, devices=devices),
        mesh=mesh,
        in_specs=(P(("slides", "row"), None, None), split, split) + (P(),) * 12,
        out_specs=(P(("slides", "row"), None), P(("slides", "row"), None)),
        check_vma=False,
    )
```
